32 devices in a mesh: groups: 2 (over x), expert: 16 (over z, y, core).
Axes of the slice: x: 2, y: 2, z: 4, core: 2. Of those that a mesh axis runs over, the one named last changes fastest.
Arguments:
- tokens: bfloat16 [2, 2048, 2048], P(None, ('groups', 'expert')), parts along dimension 1, may hold values from -6 to 6
- w_gate: bfloat16 [16, 2048, 768], P('expert'), may hold values from -0.125 to 0.125
- w_up: bfloat16 [16, 2048, 768], P('expert'), may hold values from -0.125 to 0.125
- w_down: bfloat16 [16, 768, 2048], P('expert'), may hold values from -0.21875 to 0.21875
- hot_gate: bfloat16 [2, 2048, 768], P(None, None, 'expert'), may hold values from -0.125 to 0.125
- hot_up: bfloat16 [2, 2048, 768], P(None, None, 'expert'), may hold values from -0.125 to 0.125
- hot_down: bfloat16 [2, 2048, 768], P(None, None, 'expert'), may hold values from -0.21875 to 0.21875
- cold_routes: int32 [2, 2048, 7], P(None, ('groups', 'expert')), parts along dimension 1, may hold values from 0 to 15, all different within a row; in each aligned block of 64 rows (0 to 63, 64 to 127, ..., all dimensions but the last counted through in order) at most 43 rows name the same one
- hot_pick: int32 [2, 2048], P(None, ('groups', 'expert')), parts along dimension 1, may hold values from 0 to 1, as said below
- gates: float32 [2, 2048, 8], P(None, ('groups', 'expert')), parts along dimension 1, may hold values from 0.1 to 1
Outputs:
- mixed: bfloat16 [2, 2048, 2048], P(None, ('groups', 'expert')), parts along dimension 1
The draws below stay inside these ranges and needn't reach their ends.
There are 2 independent parts, one for each index of `groups`. The reference program is written for one: setup_inputs(seed, part) draws one part's arguments, and reference() takes and returns one part's arrays. A program takes and returns all parts, laid end to end along the dimension named above; an argument that names none is the same for every part. Nothing has to cross between parts.
Inputs may be any that keep to these rules, and one draw needn't show every extreme that they name: `hot_pick`: in each aligned block of 64 tokens of one micro-batch, each hot expert is picked by exactly 32 tokens. `cold_routes`: A token names 8 - 1 different cold experts; in each aligned block of 64 tokens of one micro-batch no cold expert is named more than 43 times.
All inputs are finite; a program needn't handle non-finite values.
Results may differ from the reference program's by a relative error of at most 0.0058.
Values may be sent and summed in bfloat16 or wider, within the bound.
A program may use at most 128 MiB of HBM per device.

```python
import math
import jax
import jax.numpy as jnp
import numpy as np
from jax import lax

D = 2048
FF = 768
TOP = 8
HOT = 2
MB = 2
TOK_DEV = 64
COLD = 16
TOKENS = 1024
CAP = 43
N_EXPERT = 16


def draw_hot_pick(key, part):
    blocks = MB * TOKENS // TOK_DEV
    keys = jax.random.split(key, blocks)

    def one_block(block_key):
        return jax.random.permutation(block_key, TOK_DEV)
    orders = jax.vmap(one_block)(keys)
    return (orders % HOT).astype(jnp.int32).reshape(MB, TOKENS)


def block_scale(own_key, extent, cuts, smallest, top_value):
    def one(position, shards_of):
        heights = jax.random.uniform(jax.random.fold_in(jax.random.fold_in(own_key, 6), position), (shards_of,), jnp.float32, smallest / len(cuts), top_value / len(cuts))
        return jnp.repeat(jnp.exp(heights), extent[position] // shards_of).reshape((-1,) + (1,) * (len(extent) - position - 1))

    level = one(*cuts[0])
    for cut in cuts[1:]:
        level = level * one(*cut)
    return level


def deal_out(own_key, own, number, rows, amount, top, most, slope):
    sequence = jax.random.permutation(own_key, amount)
    packed, common = shares(amount, rows * top, most, slope, True), shares(amount, rows * top, most, slope, False)
    places = jnp.arange(amount)

    def named(sizes, offset_by):
        used = int((sizes > 0).sum())
        fixed = max(1, used // 4)
        moved = fixed + (places - fixed + offset_by * (used - fixed)) % max(1, amount - fixed)
        return jnp.zeros((amount,), jnp.int32).at[sequence[jnp.where(places < fixed, places, moved)]].set(jnp.asarray(sizes, jnp.int32))

    sizes = jnp.where(number % 4 == 0, named(packed, number // 4), named(common, number - number // 4 - 1))
    mixed = jax.random.permutation(jax.random.fold_in(own, 3), amount)
    source_of, taker = mixed[0:amount // 2 * 2:2], mixed[1:amount // 2 * 2:2]
    room = jnp.minimum(sizes[source_of] - 1, most - sizes[taker]) // 2
    room = jnp.where((source_of == sequence[0]) | (taker == sequence[0]) | (sizes[taker] == 0), 0, jnp.maximum(room, 0))
    moved = jax.random.randint(jax.random.fold_in(own, 4), (amount // 2,), 0, 1 << 20) % (room + 1)
    sizes = sizes.at[source_of].add(-moved).at[taker].add(moved)
    labels = jnp.searchsorted(jnp.cumsum(sizes), jnp.arange(rows * top), side="right").astype(jnp.int32)
    table = labels.reshape(top, rows).T
    table = table[jax.random.permutation(jax.random.fold_in(own, 1), rows)]
    offset_by = jax.random.randint(jax.random.fold_in(own, 2), (rows, 1), 0, top)
    return jnp.take_along_axis(table, (jnp.arange(top)[None, :] + offset_by) % top, axis=1)


def shares(number_of, total, reach, slope, full):
    loads = [(1 << 20) // math.isqrt(rank ** slope) + 1 for rank in range(1, number_of + 1)]
    largest = reach if full else min(reach, max(-(-total // number_of), total * loads[0] // sum(loads)))
    least = 1 if total - largest >= number_of - 1 else 0
    holding, spare = [largest] + [least] * (number_of - 1), total - largest - least * (number_of - 1)
    while spare > 0:
        candidates = [i for i in range(1, number_of) if holding[i] < largest] or [i for i in range(1, number_of) if holding[i] < reach]
        mass, budget = sum([loads[i] for i in candidates]), spare
        for i in candidates:
            more = min(reach - holding[i], max(1, budget * loads[i] // mass), spare)
            holding[i] = holding[i] + more
            spare = spare - more
    return np.array(holding)


def noise(stream_key, shape, width, most, cuts=(), kind=jnp.bfloat16):
    loudness = block_scale(stream_key, shape, cuts, -0.22, 0.18) if cuts else 1.0
    array = jax.random.normal(stream_key, shape, jnp.float32) * width * loudness
    return jnp.minimum(jnp.maximum(array, -most), most).astype(kind)


def setup_inputs(seed: int = 0, part: int = 0) -> dict:
    seeds = jax.random.split(jax.random.key(seed), 11)
    part_splits = jax.random.split(jax.random.fold_in(seeds[10], part), 11)
    tokens = noise(part_splits[0], (MB, TOKENS, D), 1.0, 6.0, ((1, 16),))
    w_gate = noise(seeds[1], (COLD, D, FF), D ** -0.5, 0.125, ((0, 16),))
    w_up = noise(seeds[2], (COLD, D, FF), D ** -0.5, 0.125, ((0, 16),))
    w_down = noise(seeds[3], (COLD, FF, D), FF ** -0.5, 0.21875, ((0, 16),))
    hot_gate = noise(seeds[4], (HOT, D, FF), D ** -0.5, 0.125, ((2, 16),))
    hot_up = noise(seeds[5], (HOT, D, FF), D ** -0.5, 0.125, ((2, 16),))
    hot_down = noise(seeds[6], (HOT, D, FF), FF ** -0.5, 0.21875, ((2, 16),))
    cold_routes_keys = jax.random.split(jax.random.fold_in(part_splits[7], 1), MB * TOKENS // TOK_DEV)
    cold_routes_turns = jax.random.permutation(jax.random.fold_in(part_splits[7], 3), MB * TOKENS // TOK_DEV)
    cold_routes = jax.vmap(lambda own, number: deal_out(jax.random.fold_in(part_splits[7], 2), own, number, TOK_DEV, COLD, TOP - 1, CAP, 2))(cold_routes_keys, cold_routes_turns).reshape((MB, TOKENS, TOP - 1))
    hot_pick = draw_hot_pick(jax.random.fold_in(jax.random.fold_in(seeds[10], part), 71), part)
    gates = jnp.clip(jnp.exp(math.log(1.0) - 2.3025851 * jax.random.uniform(part_splits[9], (MB, TOKENS, TOP), jnp.float32) ** block_scale(part_splits[9], (MB, TOKENS, TOP), ((1, 16),), -0.2, 0.2)), 0.1, 1.0)
    return {"tokens": tokens, "w_gate": w_gate, "w_up": w_up, "w_down": w_down, "hot_gate": hot_gate, "hot_up": hot_up, "hot_down": hot_down, "cold_routes": cold_routes, "hot_pick": hot_pick, "gates": gates}


def expert_rows(rows_in, gate_one, up_one, down_one):
    gate = jnp.dot(rows_in, gate_one, preferred_element_type=jnp.float32)
    upward = jnp.dot(rows_in, up_one, preferred_element_type=jnp.float32)
    hidden = (jax.nn.silu(gate) * upward).astype(jnp.bfloat16)
    return jnp.dot(hidden, down_one, preferred_element_type=jnp.float32).astype(jnp.bfloat16)


def reference(tokens, w_gate, w_up, w_down, hot_gate, hot_up, hot_down, cold_routes, hot_pick, gates):
    all_rows = MB * TOKENS
    picks = TOP - 1
    flat = tokens.reshape(all_rows, D)
    expert = cold_routes.reshape(all_rows * picks)
    owner = jnp.repeat(jnp.arange(all_rows, dtype=jnp.int32), picks)
    weight = gates[:, :, 1:].reshape(all_rows * picks)
    bound = MB * N_EXPERT * CAP

    def visit(carry, number):
        chosen = expert == number
        found = jnp.nonzero(chosen, size=bound, fill_value=0)[0].astype(jnp.int32)
        live = jnp.arange(bound, dtype=jnp.int32) < jnp.sum(chosen.astype(jnp.int32))
        rows_at = owner[found]
        result = expert_rows(flat[rows_at], w_gate[number], w_up[number], w_down[number])
        scaled = jnp.where(live, weight[found], jnp.zeros_like(weight[found]))[:, None] * result.astype(jnp.float32)
        return carry.at[rows_at].add(scaled), None

    total = jnp.zeros((all_rows, D), jnp.float32)
    total, unused = lax.scan(visit, total, jnp.arange(COLD, dtype=jnp.int32))
    pick_flat = hot_pick.reshape(all_rows)
    share = all_rows // HOT
    hot_gate_row = gates[:, :, 0].reshape(all_rows)
    for number in range(HOT):
        found = jnp.nonzero(pick_flat == number, size=share, fill_value=0)[0].astype(jnp.int32)
        result = expert_rows(flat[found], hot_gate[number], hot_up[number], jnp.transpose(hot_down[number]))
        total = total.at[found].add(hot_gate_row[found][:, None] * result.astype(jnp.float32))
    return total.astype(jnp.bfloat16).reshape(MB, TOKENS, D)
```

```python
import jax
import jax.numpy as jnp
from jax import lax
from jax.sharding import PartitionSpec as P


def coefficients(cold_routes, hot_pick, gates, width, hot):
    cold = cold_routes[:, :, None] == jnp.arange(width, dtype=jnp.int32)
    cold = jnp.sum(jnp.where(cold, gates[:, 1:, None], 0.0), axis=1)
    warm = hot_pick[:, None] == jnp.arange(hot, dtype=jnp.int32)
    warm = jnp.where(warm, gates[:, :1], 0.0)
    return jnp.concatenate([cold, warm], axis=1).T


def shards(tokens, w_gate, w_up, w_down, hot_gate, hot_up, hot_down, cold_routes, hot_pick, gates):
    width = lax.axis_size("expert")
    me = lax.axis_index("expert")
    micro_count, local_tokens, model = tokens.shape
    hot = hot_gate.shape[0]
    units = w_gate.shape[2]
    part = hot_gate.shape[2]

    gate_w = jnp.concatenate([w_gate[0]] + [hot_gate[h] for h in range(hot)], axis=1)
    up_w = jnp.concatenate([w_up[0]] + [hot_up[h] for h in range(hot)], axis=1)
    down_w = jnp.concatenate([w_down[0]] + [hot_down[h].T for h in range(hot)], axis=0)

    table = coefficients(
        cold_routes.reshape(micro_count * local_tokens, -1),
        hot_pick.reshape(-1),
        gates.reshape(micro_count * local_tokens, -1),
        width,
        hot,
    )
    table = lax.all_gather(table, "expert", axis=0)
    cold_c = lax.dynamic_index_in_dim(table, me, axis=1, keepdims=False)
    hot_c = table[:, width:]

    outs = []
    for micro in range(micro_count):
        rows = lax.all_gather(tokens[micro], "expert", axis=0, tiled=True)
        span = slice(micro * local_tokens, (micro + 1) * local_tokens)
        scale = [jnp.broadcast_to(cold_c[:, span].reshape(-1, 1), (width * local_tokens, units))]
        for h in range(hot):
            scale.append(
                jnp.broadcast_to(hot_c[:, h, span].reshape(-1, 1), (width * local_tokens, part))
            )
        scale = jnp.concatenate(scale, axis=1)
        gate = jnp.dot(rows, gate_w, preferred_element_type=jnp.float32)
        upward = jnp.dot(rows, up_w, preferred_element_type=jnp.float32)
        hidden = (jax.nn.silu(gate) * upward * scale).astype(jnp.bfloat16)
        mixed = jnp.dot(hidden, down_w, preferred_element_type=jnp.float32).astype(jnp.bfloat16)
        outs.append(lax.psum_scatter(mixed, "expert", scatter_dimension=0, tiled=True))
    return jnp.stack(outs)


def solution(mesh):
    in_specs = (
        P(None, ("groups", "expert"), None),
        P("expert", None, None),
        P("expert", None, None),
        P("expert", None, None),
        P(None, None, "expert"),
        P(None, None, "expert"),
        P(None, None, "expert"),
        P(None, ("groups", "expert"), None),
        P(None, ("groups", "expert")),
        P(None, ("groups", "expert"), None),
    )
    out_specs = P(None, ("groups", "expert"), None)
    return jax.shard_map(shards, mesh=mesh, in_specs=in_specs, out_specs=out_specs, check_vma=False)
```

```python
import functools

import jax
import jax.numpy as jnp
from jax import lax
from jax.experimental import pallas as pl
from jax.experimental.pallas import tpu as pltpu
from jax.sharding import PartitionSpec as P

TOP = 8
HOT = 2


def expert_rows(rows_in, weights):
    leading = rows_in.shape[:-1]
    flat_rows = rows_in.reshape(-1, rows_in.shape[-1])
    gate = jnp.dot(flat_rows, weights[0], preferred_element_type=jnp.float32)
    upward = jnp.dot(flat_rows, weights[1], preferred_element_type=jnp.float32)
    hidden = (jax.nn.silu(gate) * upward).astype(jnp.bfloat16)
    result = jnp.dot(hidden, weights[2], preferred_element_type=jnp.float32).astype(jnp.bfloat16)
    return result.reshape(leading + (result.shape[-1],))


def slot_table(routes_block, axis_width, capacity):
    expert = routes_block.reshape(-1)
    total_count = expert.shape[0]
    onehot = (expert[:, None] == jnp.arange(axis_width, dtype=jnp.int32)[None, :]).astype(jnp.int32)
    before = jnp.cumsum(onehot, axis=0) - onehot
    slot_rank = jnp.sum(before * onehot, axis=1)
    slot_place = expert * capacity + slot_rank
    target = jnp.arange(axis_width * capacity, dtype=jnp.int32)
    matched = slot_place[None, :] == target[:, None]
    filled = jnp.any(matched, axis=1)
    source = jnp.sum(
        jnp.where(matched, jnp.arange(total_count, dtype=jnp.int32)[None, :], 0), axis=1
    )
    return (slot_place, source, filled)


def routed(tokens, w_gate, w_up, w_down, hot_gate, hot_up, hot_down, cold_routes, hot_pick, gates):
    axis_width = lax.axis_size("expert")
    micro_count, local_tokens, model_width = tokens.shape
    picks = TOP - 1
    capacity = local_tokens * picks * 3 // (2 * axis_width) + 1
    own_weights = (w_gate[0], w_up[0], w_down[0])
    outbound = []
    tables = []
    for micro in range(micro_count):
        slot_place, source, filled = slot_table(cold_routes[micro], axis_width, capacity)
        rows_out = tokens[micro][source // picks]
        rows_out = jnp.where(filled[:, None], rows_out, jnp.zeros_like(rows_out))
        outbound.append(rows_out.reshape(axis_width, capacity, model_width))
        tables.append(slot_place)
    joined = jnp.concatenate(outbound, axis=1)
    back_all = lax.all_to_all(
        expert_rows(
            lax.all_to_all(joined, "expert", split_axis=0, concat_axis=0, tiled=True), own_weights
        ),
        "expert",
        split_axis=0,
        concat_axis=0,
        tiled=True,
    )
    returned = [
        back_all[:, micro * capacity : (micro + 1) * capacity] for micro in range(micro_count)
    ]
    cold_parts = []
    for micro in range(micro_count):
        picked = returned[micro].reshape(axis_width * capacity, model_width)[tables[micro]]
        picked = picked.reshape(local_tokens, picks, model_width).astype(jnp.float32)
        cold_parts.append(jnp.sum(picked * gates[micro, :, 1:, None], axis=1))
    cold_total = jnp.stack(cold_parts)
    all_rows = micro_count * local_tokens
    flat = tokens.reshape(all_rows, model_width)
    order = jnp.argsort(hot_pick.reshape(all_rows), stable=True)
    share = all_rows // HOT
    grouped = flat[order].reshape(HOT, share, model_width)
    gate = jnp.einsum(
        "hsd,hdf->hsf",
        grouped,
        lax.all_gather(hot_gate, "expert", axis=2, tiled=True),
        preferred_element_type=jnp.float32,
    )
    upward = jnp.einsum(
        "hsd,hdf->hsf",
        grouped,
        lax.all_gather(hot_up, "expert", axis=2, tiled=True),
        preferred_element_type=jnp.float32,
    )
    hidden = (jax.nn.silu(gate) * upward).astype(jnp.bfloat16)
    hot_sum = jnp.einsum(
        "hsf,hdf->hsd",
        hidden,
        lax.all_gather(hot_down, "expert", axis=2, tiled=True),
        preferred_element_type=jnp.float32,
    )
    sorted_out = hot_sum.astype(jnp.bfloat16).reshape(all_rows, model_width)
    inverse = jnp.argsort(order)
    hot_out = sorted_out[inverse].astype(jnp.float32) * gates[:, :, 0].reshape(all_rows)[:, None]
    total = hot_out.reshape(micro_count, local_tokens, model_width) + cold_total
    return total.astype(jnp.bfloat16)


QUARTERS = 4
ROOM = 56 * 2**20


def column(row):
    rows = row.shape[1]
    down = lax.broadcasted_iota(jnp.int32, (rows, rows), 0)
    across = lax.broadcasted_iota(jnp.int32, (rows, rows), 1)
    return jnp.sum(jnp.where(down == across, row, 0.0), axis=1, keepdims=True)


def fused(
    n, hot, part, tok, ct, wg_in, wu_in, wd_in, wh_in, out,
    xs, keep, sc, rc, sy, ry, sz, rz, wg, wu, wd, wh, hid, hhid, cs,
    wsem, tsem, cts, ctr, up_s, down_s, z_r, y_s, y_r, c_s, c_r,
    rc_s, rc_r, ry_s, ry_r, rz_s, rz_r,
):
    nz = n // 4
    rows, model = tok.shape
    units = wg.shape[1]
    pad = hhid.shape[1]
    piece = rows // QUARTERS
    me = lax.axis_index("expert")
    c = lax.rem(me, 2)
    y = lax.rem(lax.div(me, 2), 2)
    z = lax.div(me, 4)
    own = y * 2 + c
    side = (1 - y) * 2 + c
    peer_y = z * 4 + side
    peer_c = z * 4 + y * 2 + (1 - c)

    def remote(src, dst, send, recv, device):
        return pltpu.make_async_remote_copy(
            src_ref=src, dst_ref=dst, send_sem=send, recv_sem=recv,
            device_id={"expert": device}, device_id_type=pl.DeviceIdType.MESH,
        )

    loads = [
        pltpu.make_async_copy(src, dst, wsem.at[i])
        for i, (src, dst) in enumerate(((wg_in, wg), (wu_in, wu), (wd_in, wd), (wh_in, wh)))
    ]
    first = pltpu.make_async_copy(tok, xs.at[z, own], tsem)
    first.start()
    for load in loads:
        load.start()

    barrier = pltpu.get_barrier_semaphore()

    @pl.loop(1, n)
    def _(i):
        pl.semaphore_signal(
            barrier, inc=1, device_id={"expert": lax.rem(me + i, n)},
            device_id_type=pl.DeviceIdType.MESH,
        )

    pl.semaphore_wait(barrier, n - 1)

    def ct_copy(i):
        peer = lax.rem(me + i, n)
        return remote(ct.at[peer], cs.at[me], cts.at[i], ctr.at[me], peer)

    def go_up(p):
        return remote(xs.at[p, own], xs.at[p, own], up_s.at[p], z_r.at[p], me + 4)

    def go_down(p):
        return remote(xs.at[p, own], xs.at[p, own], down_s.at[p], z_r.at[p], me - 4)

    def go_y(p):
        return remote(xs.at[p, own], xs.at[p, own], y_s.at[p], y_r.at[p], peer_y)

    def go_c(p, which):
        slot = own if which == 0 else side
        return remote(
            xs.at[p, slot], xs.at[p, slot], c_s.at[p, which], c_r.at[p, which], peer_c
        )

    def spread(p):
        @pl.when((p <= z) & (z + 1 < nz))
        def _():
            go_up(p).start()

        @pl.when((p >= z) & (z > 0))
        def _():
            go_down(p).start()

        go_y(p).start()
        go_c(p, 0).start()

    def landed(p):
        remote(xs.at[p, own], xs.at[p, own], up_s.at[p], z_r.at[p], me).wait_recv()
        spread(p)

    def plane(s):
        near = jnp.minimum(z, nz - 1 - z)
        step = lax.div(s + 1, 2)
        both = jnp.where(lax.rem(s, 2) == 1, z - step, z + step)
        far = jnp.where(z * 2 < nz, s, nz - 1 - s)
        return jnp.where(s <= 2 * near, both, far)

    def share(p, j, q):
        span = pl.ds(pl.multiple_of(q * piece, piece), piece)
        return remote(
            sc.at[p, j, span], rc.at[p, j, span], rc_s.at[p, j, q], rc_r.at[p, j, q], peer_c
        )

    def share_y(p, q):
        span = pl.ds(pl.multiple_of(q * piece, piece), piece)
        return remote(sy.at[p, span], ry.at[p, span], ry_s.at[p, q], ry_r.at[p, q], peer_y)

    def share_z(way, p, q):
        span = pl.ds(pl.multiple_of(q * piece, piece), piece)
        return remote(
            sz.at[way, p, span], rz.at[way, p, span], rz_s.at[way, p, q], rz_r.at[way, p, q],
            jnp.where(way == 0, me + 4, me - 4),
        )

    def compute(p):
        wide = 256 if units % 256 == 0 else units
        x = xs.at[p]
        cold_c = jnp.concatenate([column(cs[p * 4 + j, 0:1, :]) for j in range(4)], axis=0)

        @pl.loop(0, units // wide)
        def _(k):
            cols = pl.ds(pl.multiple_of(k * wide, wide), wide)
            v = x[...].reshape(4 * rows, model)
            g = jnp.dot(v, wg[:, cols], preferred_element_type=jnp.float32)
            u = jnp.dot(v, wu[:, cols], preferred_element_type=jnp.float32)
            hid[:, cols] = (g / (1.0 + jnp.exp(-g)) * u).astype(jnp.bfloat16)

        v = x[...].reshape(4 * rows, model)
        gu = jnp.dot(v, wh[:, : 2 * pad], preferred_element_type=jnp.float32)
        g, u = gu[:, :pad], gu[:, pad:]
        lane = lax.broadcasted_iota(jnp.int32, (rows, pad), 1)
        warm = []
        for j in range(4):
            scale = jnp.zeros((rows, pad), jnp.float32)
            for h in range(hot):
                weight = column(cs[p * 4 + j, 1 + h : 2 + h, :])
                scale = jnp.where((lane >= h * part) & (lane < (h + 1) * part), weight, scale)
            warm.append(scale)
        warm = jnp.concatenate(warm, axis=0)
        hhid[...] = (g / (1.0 + jnp.exp(-g)) * u * warm).astype(jnp.bfloat16)

        tile = 512 if model % 512 == 0 else model

        @pl.loop(0, model // tile)
        def _(k):
            cols = pl.ds(pl.multiple_of(k * tile, tile), tile)
            r = jnp.dot(hid[...], wd[:, cols], preferred_element_type=jnp.float32)
            r = r.astype(jnp.bfloat16).astype(jnp.float32) * cold_c
            r = r + lax.dot_general(
                hhid[...], wh[cols, 2 * pad :], (((1,), (1,)), ((), ())),
                preferred_element_type=jnp.float32,
            )
            for j in range(2):
                low = r[2 * j * rows : (2 * j + 1) * rows]
                high = r[(2 * j + 1) * rows : (2 * j + 2) * rows]
                keep[p, j, :, cols] = jnp.where(c == 0, low, high)
                sc[p, j, :, cols] = jnp.where(c == 0, high, low).astype(jnp.bfloat16)

    def y_step(p):
        @pl.loop(0, QUARTERS)
        def _(q):
            span = pl.ds(pl.multiple_of(q * piece, piece), piece)
            share(p, 1 - y, q).wait_recv()
            total = keep[p, 1 - y, span, :] + rc[p, 1 - y, span, :].astype(jnp.float32)
            sy[p, span, :] = total.astype(jnp.bfloat16)
            share_y(p, q).start()

        @pl.loop(0, QUARTERS)
        def _(q):
            span = pl.ds(pl.multiple_of(q * piece, piece), piece)
            share(p, y, q).wait_recv()
            keep[p, y, span, :] += rc[p, y, span, :].astype(jnp.float32)

    def z_step(k):
        @pl.loop(0, 2)
        def _(turn):
            way = jnp.where(z * 2 < nz, turn, 1 - turn)
            p = jnp.where(way == 0, k, nz - 1 - k)
            active = jnp.where(way == 0, z < k, z > nz - 1 - k)
            fed = jnp.where(way == 0, z > 0, z < nz - 1)

            @pl.when(active)
            def _():
                @pl.loop(0, QUARTERS)
                def _(q):
                    span = pl.ds(pl.multiple_of(q * piece, piece), piece)
                    share_y(p, q).wait_recv()
                    keep[p, y, span, :] += ry[p, span, :].astype(jnp.float32)

                    @pl.when(fed)
                    def _():
                        share_z(way, p, q).wait_recv()
                        keep[p, y, span, :] += rz[way, p, span, :].astype(jnp.float32)

                    sz[way, p, span, :] = keep[p, y, span, :].astype(jnp.bfloat16)
                    share_z(way, p, q).start()

    first.wait()
    spread(z)

    @pl.loop(1, n)
    def _(i):
        ct_copy(i).start()

    cs[me] = ct[me]

    @pl.loop(0, nz)
    def _(s):
        p = plane(s)

        @pl.when((s + 1 < nz) & (z - s - 1 >= 0))
        def _():
            landed(z - s - 1)

        @pl.when((s + 1 < nz) & (z + s + 1 < nz))
        def _():
            landed(z + s + 1)

        go_y(p).wait_recv()
        go_c(p, 1).start()

        @pl.when(s == 0)
        def _():
            for load in loads:
                load.wait()

            @pl.loop(1, n)
            def _(i):
                other = lax.rem(me + i, n)
                remote(ct.at[other], cs.at[other], cts.at[i], ctr.at[other], other).wait_recv()

        go_c(p, 0).wait_recv()
        go_c(p, 1).wait_recv()
        compute(p)

        @pl.loop(0, QUARTERS)
        def _(q):
            share(p, 1 - y, q).start()

        @pl.loop(0, QUARTERS)
        def _(q):
            share(p, y, q).start()

        @pl.when(s >= 1)
        def _():
            y_step(plane(s - 1))

        @pl.when(s >= 3)
        def _():
            z_step(s - 2)

    y_step(plane(nz - 1))
    for k in range(max(1, nz - 2), nz):
        z_step(k)

    @pl.loop(0, QUARTERS)
    def _(q):
        span = pl.ds(pl.multiple_of(q * piece, piece), piece)
        share_y(z, q).wait_recv()
        keep[z, y, span, :] += ry[z, span, :].astype(jnp.float32)

        @pl.when(z > 0)
        def _():
            share_z(0, z, q).wait_recv()
            keep[z, y, span, :] += rz[0, z, span, :].astype(jnp.float32)

        @pl.when(z < nz - 1)
        def _():
            share_z(1, z, q).wait_recv()
            keep[z, y, span, :] += rz[1, z, span, :].astype(jnp.float32)

        out[span, :] = keep[z, y, span, :].astype(jnp.bfloat16)

    @pl.loop(1, n)
    def _(i):
        ct_copy(i).wait_send()

    @pl.loop(0, nz)
    def _(p):
        @pl.when((p <= z) & (z + 1 < nz))
        def _():
            go_up(p).wait_send()

        @pl.when((p >= z) & (z > 0))
        def _():
            go_down(p).wait_send()

        go_y(p).wait_send()
        go_c(p, 0).wait_send()
        go_c(p, 1).wait_send()

        @pl.loop(0, QUARTERS)
        def _(q):
            share(p, 0, q).wait_send()
            share(p, 1, q).wait_send()
            share_y(p, q).wait_send()

            @pl.when(p > z)
            def _():
                share_z(0, p, q).wait_send()

            @pl.when(p < z)
            def _():
                share_z(1, p, q).wait_send()


def scratch(n, rows, model, units, pad):
    nz = n // 4
    half, full = jnp.bfloat16, jnp.float32
    dma = pltpu.SemaphoreType.DMA
    return [
        pltpu.VMEM((nz, 4, rows, model), half),
        pltpu.VMEM((nz, 2, rows, model), full),
        pltpu.VMEM((nz, 2, rows, model), half),
        pltpu.VMEM((nz, 2, rows, model), half),
        pltpu.VMEM((nz, rows, model), half),
        pltpu.VMEM((nz, rows, model), half),
        pltpu.VMEM((2, nz, rows, model), half),
        pltpu.VMEM((2, nz, rows, model), half),
        pltpu.VMEM((model, units), half),
        pltpu.VMEM((model, units), half),
        pltpu.VMEM((units, model), half),
        pltpu.VMEM((model, 3 * pad), half),
        pltpu.VMEM((4 * rows, units), half),
        pltpu.VMEM((4 * rows, pad), half),
        pltpu.VMEM((n, 8, rows), full),
        dma((4,)), dma, dma((n,)), dma((n,)),
        dma((nz,)), dma((nz,)), dma((nz,)), dma((nz,)), dma((nz,)), dma((nz, 2)), dma((nz, 2)),
        dma((nz, 2, QUARTERS)), dma((nz, 2, QUARTERS)),
        dma((nz, QUARTERS)), dma((nz, QUARTERS)),
        dma((2, nz, QUARTERS)), dma((2, nz, QUARTERS)),
    ]


def shards(tokens, w_gate, w_up, w_down, hot_gate, hot_up, hot_down, cold_routes, hot_pick, gates):
    n = lax.axis_size("expert")
    micro_count, local_tokens, model = tokens.shape
    rows = micro_count * local_tokens
    hot, units, part = hot_gate.shape[0], w_gate.shape[2], hot_gate.shape[2]
    pad = -(-hot * part // 128) * 128
    need = rows * model * n * 9 // 2 * 2 + 3 * model * (units + pad) * 2
    if n % 4 or rows % 64 or need > ROOM or hot > 7:
        return routed(
            tokens, w_gate, w_up, w_down, hot_gate, hot_up, hot_down, cold_routes, hot_pick, gates
        )
    routes = cold_routes.reshape(rows, -1).T
    weights = gates.reshape(rows, -1).T
    chosen = routes[None] == jnp.arange(n, dtype=jnp.int32)[:, None, None]
    cold = jnp.sum(jnp.where(chosen, weights[None, 1:], 0.0), axis=1)
    warm = hot_pick.reshape(1, rows) == jnp.arange(hot, dtype=jnp.int32)[:, None]
    warm = jnp.where(warm, weights[:1], 0.0)
    table = jnp.concatenate(
        [cold[:, None], jnp.broadcast_to(warm[None], (n, hot, rows)),
         jnp.zeros((n, 7 - hot, rows), jnp.float32)], axis=1,
    )
    blank = [jnp.zeros((model, pad - hot * part), jnp.bfloat16)] if pad > hot * part else []
    joined = jnp.concatenate(
        [v for w in (hot_gate, hot_up, hot_down) for v in [w[h] for h in range(hot)] + blank],
        axis=1,
    )
    anyplace = pl.BlockSpec(memory_space=pl.ANY)
    vmem = pl.BlockSpec(memory_space=pltpu.VMEM)
    mixed = pl.pallas_call(
        functools.partial(fused, n, hot, part),
        out_shape=jax.ShapeDtypeStruct((rows, model), jnp.bfloat16),
        in_specs=[anyplace, vmem, anyplace, anyplace, anyplace, anyplace],
        out_specs=vmem,
        scratch_shapes=scratch(n, rows, model, units, pad),
        compiler_params=pltpu.CompilerParams(
            collective_id=0, has_side_effects=True, vmem_limit_bytes=64 * 2**20 - 2**17
        ),
    )(tokens.reshape(rows, model), table, w_gate[0], w_up[0], w_down[0], joined)
    return mixed.reshape(tokens.shape)


def solution(mesh):
    in_specs = (
        P(None, ("groups", "expert"), None),
        P("expert", None, None),
        P("expert", None, None),
        P("expert", None, None),
        P(None, None, "expert"),
        P(None, None, "expert"),
        P(None, None, "expert"),
        P(None, ("groups", "expert"), None),
        P(None, ("groups", "expert")),
        P(None, ("groups", "expert"), None),
    )
    out_specs = P(None, ("groups", "expert"), None)
    return jax.shard_map(shards, mesh=mesh, in_specs=in_specs, out_specs=out_specs, check_vma=False)
```

```python
import functools

import jax
import jax.numpy as jnp
from jax import lax
from jax.experimental import pallas as pl
from jax.experimental.pallas import tpu as pltpu
from jax.sharding import PartitionSpec as P

TOP = 8
HOT = 2


def expert_rows(rows_in, weights):
    leading = rows_in.shape[:-1]
    flat_rows = rows_in.reshape(-1, rows_in.shape[-1])
    gate = jnp.dot(flat_rows, weights[0], preferred_element_type=jnp.float32)
    upward = jnp.dot(flat_rows, weights[1], preferred_element_type=jnp.float32)
    hidden = (jax.nn.silu(gate) * upward).astype(jnp.bfloat16)
    result = jnp.dot(hidden, weights[2], preferred_element_type=jnp.float32).astype(jnp.bfloat16)
    return result.reshape(leading + (result.shape[-1],))


def slot_table(routes_block, axis_width, capacity):
    expert = routes_block.reshape(-1)
    total_count = expert.shape[0]
    onehot = (expert[:, None] == jnp.arange(axis_width, dtype=jnp.int32)[None, :]).astype(jnp.int32)
    before = jnp.cumsum(onehot, axis=0) - onehot
    slot_rank = jnp.sum(before * onehot, axis=1)
    slot_place = expert * capacity + slot_rank
    target = jnp.arange(axis_width * capacity, dtype=jnp.int32)
    matched = slot_place[None, :] == target[:, None]
    filled = jnp.any(matched, axis=1)
    source = jnp.sum(
        jnp.where(matched, jnp.arange(total_count, dtype=jnp.int32)[None, :], 0), axis=1
    )
    return (slot_place, source, filled)


def routed(tokens, w_gate, w_up, w_down, hot_gate, hot_up, hot_down, cold_routes, hot_pick, gates):
    axis_width = lax.axis_size("expert")
    micro_count, local_tokens, model_width = tokens.shape
    picks = TOP - 1
    capacity = local_tokens * picks * 3 // (2 * axis_width) + 1
    own_weights = (w_gate[0], w_up[0], w_down[0])
    outbound = []
    tables = []
    for micro in range(micro_count):
        slot_place, source, filled = slot_table(cold_routes[micro], axis_width, capacity)
        rows_out = tokens[micro][source // picks]
        rows_out = jnp.where(filled[:, None], rows_out, jnp.zeros_like(rows_out))
        outbound.append(rows_out.reshape(axis_width, capacity, model_width))
        tables.append(slot_place)
    joined = jnp.concatenate(outbound, axis=1)
    back_all = lax.all_to_all(
        expert_rows(
            lax.all_to_all(joined, "expert", split_axis=0, concat_axis=0, tiled=True), own_weights
        ),
        "expert",
        split_axis=0,
        concat_axis=0,
        tiled=True,
    )
    returned = [
        back_all[:, micro * capacity : (micro + 1) * capacity] for micro in range(micro_count)
    ]
    cold_parts = []
    for micro in range(micro_count):
        picked = returned[micro].reshape(axis_width * capacity, model_width)[tables[micro]]
        picked = picked.reshape(local_tokens, picks, model_width).astype(jnp.float32)
        cold_parts.append(jnp.sum(picked * gates[micro, :, 1:, None], axis=1))
    cold_total = jnp.stack(cold_parts)
    all_rows = micro_count * local_tokens
    flat = tokens.reshape(all_rows, model_width)
    order = jnp.argsort(hot_pick.reshape(all_rows), stable=True)
    share = all_rows // HOT
    grouped = flat[order].reshape(HOT, share, model_width)
    gate = jnp.einsum(
        "hsd,hdf->hsf",
        grouped,
        lax.all_gather(hot_gate, "expert", axis=2, tiled=True),
        preferred_element_type=jnp.float32,
    )
    upward = jnp.einsum(
        "hsd,hdf->hsf",
        grouped,
        lax.all_gather(hot_up, "expert", axis=2, tiled=True),
        preferred_element_type=jnp.float32,
    )
    hidden = (jax.nn.silu(gate) * upward).astype(jnp.bfloat16)
    hot_sum = jnp.einsum(
        "hsf,hdf->hsd",
        hidden,
        lax.all_gather(hot_down, "expert", axis=2, tiled=True),
        preferred_element_type=jnp.float32,
    )
    sorted_out = hot_sum.astype(jnp.bfloat16).reshape(all_rows, model_width)
    inverse = jnp.argsort(order)
    hot_out = sorted_out[inverse].astype(jnp.float32) * gates[:, :, 0].reshape(all_rows)[:, None]
    total = hot_out.reshape(micro_count, local_tokens, model_width) + cold_total
    return total.astype(jnp.bfloat16)


QUARTERS = 4
ROOM = 56 * 2**20


def column(row):
    rows = row.shape[1]
    down = lax.broadcasted_iota(jnp.int32, (rows, rows), 0)
    across = lax.broadcasted_iota(jnp.int32, (rows, rows), 1)
    return jnp.sum(jnp.where(down == across, row, 0.0), axis=1, keepdims=True)


def fused(
    n, hot, part, tok, routes, pick, gts, wg_in, wu_in, wd_in, hg_in, hu_in, hd_in, out,
    xs, keep, sc, rc, sy, ry, sz, rz, wg, wu, wd, wh, hid, hhid, cs, ct, sze, rze,
    wsem, tsem, cts, ctr, up_s, down_s, z_r, y_s, y_r, c_s, c_r,
    rc_s, rc_r, ry_s, ry_r, rz_s, rz_r, eu_s, ed_s, e_r, ez_s, ez_r,
):
    nz = n // 4
    rows, model = tok.shape
    units = wg.shape[1]
    pad = hhid.shape[1]
    piece = rows // QUARTERS
    me = lax.axis_index("expert")
    c = lax.rem(me, 2)
    y = lax.rem(lax.div(me, 2), 2)
    z = lax.div(me, 4)
    own = y * 2 + c
    side = (1 - y) * 2 + c
    peer_y = z * 4 + side
    peer_c = z * 4 + y * 2 + (1 - c)

    def remote(src, dst, send, recv, device):
        return pltpu.make_async_remote_copy(
            src_ref=src, dst_ref=dst, send_sem=send, recv_sem=recv,
            device_id={"expert": device}, device_id_type=pl.DeviceIdType.MESH,
        )

    loads = [
        pltpu.make_async_copy(src, dst, wsem.at[i])
        for i, (src, dst) in enumerate((
            *(
                (src.at[h], wh.at[pl.ds(t * pad + h * part, part)])
                for t, src in enumerate((hg_in, hu_in, hd_in)) for h in range(hot)
            ),
            (wg_in, wg), (wu_in, wu), (wd_in, wd),
        ))
    ]
    first = pltpu.make_async_copy(tok, xs.at[z, own], tsem)
    first.start()
    for load in loads:
        load.start()

    barrier = pltpu.get_barrier_semaphore()

    @pl.loop(1, n)
    def _(i):
        pl.semaphore_signal(
            barrier, inc=1, device_id={"expert": lax.rem(me + i, n)},
            device_id_type=pl.DeviceIdType.MESH,
        )

    pl.semaphore_wait(barrier, n - 1)

    def ct_copy(i):
        peer = lax.rem(me + i, n)
        return remote(ct.at[peer], cs.at[me], cts.at[i], ctr.at[me], peer)

    def go_up(p):
        return remote(xs.at[p, own], xs.at[p, own], up_s.at[p], z_r.at[p], me + 4)

    def go_down(p):
        return remote(xs.at[p, own], xs.at[p, own], down_s.at[p], z_r.at[p], me - 4)

    def go_y(p):
        return remote(xs.at[p, own], xs.at[p, own], y_s.at[p], y_r.at[p], peer_y)

    def rest_y(p):
        rest = xs.at[p, own, pl.ds(piece, rows - piece)]
        return remote(rest, rest, y_s.at[p], y_r.at[p], peer_y)

    def edge(p, send, device):
        lead = xs.at[p, side, pl.ds(0, piece)]
        return remote(lead, lead, send.at[p], e_r.at[p], device)

    def spread_edge(p):
        @pl.when((p <= z) & (z + 1 < nz))
        def _():
            edge(p, eu_s, me + 4).start()

        @pl.when((p >= z) & (z > 0))
        def _():
            edge(p, ed_s, me - 4).start()

    def landed_edge(p):
        edge(p, eu_s, me).wait_recv()
        spread_edge(p)

    def go_c(p, which):
        slot = own if which == 0 else side
        return remote(
            xs.at[p, slot], xs.at[p, slot], c_s.at[p, which], c_r.at[p, which], peer_c
        )

    def spread(p):
        @pl.when((p <= z) & (z + 1 < nz))
        def _():
            go_up(p).start()

        @pl.when((p >= z) & (z > 0))
        def _():
            go_down(p).start()

    def landed(p):
        remote(xs.at[p, own], xs.at[p, own], up_s.at[p], z_r.at[p], me).wait_recv()
        spread(p)
        rest_y(p).start()
        go_c(p, 0).start()

    def plane(s):
        near = jnp.minimum(z, nz - 1 - z)
        step = lax.div(s + 1, 2)
        both = jnp.where(lax.rem(s, 2) == 1, z - step, z + step)
        far = jnp.where(z * 2 < nz, s, nz - 1 - s)
        return jnp.where(s <= 2 * near, both, far)

    def share(p, j, q):
        span = pl.ds(pl.multiple_of(q * piece, piece), piece)
        return remote(
            sc.at[p, j, span], rc.at[p, j, span], rc_s.at[p, j, q], rc_r.at[p, j, q], peer_c
        )

    def share_y(p, q):
        span = pl.ds(pl.multiple_of(q * piece, piece), piece)
        return remote(sy.at[p, span], ry.at[p, span], ry_s.at[p, q], ry_r.at[p, q], peer_y)

    def share_z(way, p, q):
        span = pl.ds(pl.multiple_of(q * piece, piece), piece)
        return remote(
            sz.at[way, p, span], rz.at[way, p, span], rz_s.at[way, p, q], rz_r.at[way, p, q],
            jnp.where(way == 0, me + 4, me - 4),
        )

    def compute(p):
        wide = 256 if units % 256 == 0 else units
        x = xs.at[p]
        cold_c = jnp.concatenate([column(cs[p * 4 + j, 0:1, :]) for j in range(4)], axis=0)

        @pl.loop(0, units // wide)
        def _(k):
            cols = pl.ds(pl.multiple_of(k * wide, wide), wide)
            v = x[...].reshape(4 * rows, model)
            g = jnp.dot(v, wg[:, cols], preferred_element_type=jnp.float32)
            u = jnp.dot(v, wu[:, cols], preferred_element_type=jnp.float32)
            hid[:, cols] = (g / (1.0 + jnp.exp(-g)) * u).astype(jnp.bfloat16)

        v = x[...].reshape(4 * rows, model)
        gu = lax.dot_general(
            v, wh[: 2 * pad, :], (((1,), (1,)), ((), ())), preferred_element_type=jnp.float32
        )
        g, u = gu[:, :pad], gu[:, pad:]
        lane = lax.broadcasted_iota(jnp.int32, (rows, pad), 1)
        warm = []
        for j in range(4):
            scale = jnp.zeros((rows, pad), jnp.float32)
            for h in range(hot):
                weight = column(cs[p * 4 + j, 1 + h : 2 + h, :])
                scale = jnp.where((lane >= h * part) & (lane < (h + 1) * part), weight, scale)
            warm.append(scale)
        warm = jnp.concatenate(warm, axis=0)
        hhid[...] = (g / (1.0 + jnp.exp(-g)) * u * warm).astype(jnp.bfloat16)

        tile = 512 if model % 512 == 0 else model

        @pl.loop(0, model // tile)
        def _(k):
            cols = pl.ds(pl.multiple_of(k * tile, tile), tile)
            r = jnp.dot(hid[...], wd[:, cols], preferred_element_type=jnp.float32)
            r = r.astype(jnp.bfloat16).astype(jnp.float32) * cold_c
            r = r + jnp.dot(hhid[...], wh[2 * pad :, cols], preferred_element_type=jnp.float32)
            for j in range(2):
                low = r[2 * j * rows : (2 * j + 1) * rows]
                high = r[(2 * j + 1) * rows : (2 * j + 2) * rows]
                keep[p, j, :, cols] = jnp.where(c == 0, low, high)
                sc[p, j, :, cols] = jnp.where(c == 0, high, low).astype(jnp.bfloat16)

    def y_step(p):
        share(p, 1 - y, 0).wait_recv()
        keep[p, 1 - y, 0:piece, :] += rc[p, 1 - y, 0:piece, :].astype(jnp.float32)

        @pl.loop(1, QUARTERS)
        def _(q):
            span = pl.ds(pl.multiple_of(q * piece, piece), piece)
            share(p, 1 - y, q).wait_recv()
            total = keep[p, 1 - y, span, :] + rc[p, 1 - y, span, :].astype(jnp.float32)
            sy[p, span, :] = total.astype(jnp.bfloat16)
            share_y(p, q).start()

        @pl.loop(0, QUARTERS)
        def _(q):
            span = pl.ds(pl.multiple_of(q * piece, piece), piece)
            share(p, y, q).wait_recv()
            keep[p, y, span, :] += rc[p, y, span, :].astype(jnp.float32)

    def share_edge(way, p):
        return remote(
            sze.at[way, p], rze.at[way, p], ez_s.at[way, p], ez_r.at[way, p],
            jnp.where(way == 0, me + 4, me - 4),
        )

    def z_step(k):
        @pl.loop(0, 2)
        def _(turn):
            way = jnp.where(z * 2 < nz, turn, 1 - turn)
            p = jnp.where(way == 0, k, nz - 1 - k)
            active = jnp.where(way == 0, z < k, z > nz - 1 - k)
            fed = jnp.where(way == 0, z > 0, z < nz - 1)

            @pl.when(active)
            def _():
                @pl.when(fed)
                def _():
                    share_edge(way, p).wait_recv()
                    keep[p, 1 - y, 0:piece, :] += rze[way, p].astype(jnp.float32)

                sze[way, p] = keep[p, 1 - y, 0:piece, :].astype(jnp.bfloat16)
                share_edge(way, p).start()

                @pl.loop(0, QUARTERS)
                def _(q):
                    span = pl.ds(pl.multiple_of(q * piece, piece), piece)

                    @pl.when(q > 0)
                    def _():
                        share_y(p, q).wait_recv()
                        keep[p, y, span, :] += ry[p, span, :].astype(jnp.float32)

                    @pl.when(fed)
                    def _():
                        share_z(way, p, q).wait_recv()
                        keep[p, y, span, :] += rz[way, p, span, :].astype(jnp.float32)

                    sz[way, p, span, :] = keep[p, y, span, :].astype(jnp.bfloat16)
                    share_z(way, p, q).start()

    first.wait()
    spread(z)
    go_y(z).start()
    go_c(z, 0).start()

    if pad > hot * part:
        for t in range(3):
            blank = wh.at[pl.ds(t * pad + hot * part, pad - hot * part)]
            blank[...] = jnp.zeros_like(blank)

    ct[...] = jnp.zeros_like(ct)
    micros = gts.shape[0]

    def joined(parts):
        return jnp.concatenate(parts, axis=1)

    warm_row = joined([gts[m, 0:1, :] for m in range(micros)])
    chosen = joined([pick[m : m + 1, :] for m in range(micros)])
    named = [
        (
            joined([routes[k, m : m + 1, :] for m in range(micros)]),
            joined([gts[m, k + 1 : k + 2, :] for m in range(micros)]),
        )
        for k in range(routes.shape[0])
    ]

    def row(e):
        return sum(jnp.where(route == e, weight, 0.0) for route, weight in named)

    for e in range(n):
        ct[e, 0:1, :] = row(e)
        for h in range(hot):
            ct[e, 1 + h : 2 + h, :] = jnp.where(chosen == h, warm_row, 0.0)

    @pl.loop(1, n)
    def _(i):
        ct_copy(i).start()

    cs[me] = ct[me]

    @pl.loop(0, nz)
    def _(s):
        p = plane(s)

        @pl.when((s + 1 < nz) & (z - s - 1 >= 0))
        def _():
            landed(z - s - 1)

        @pl.when((s + 1 < nz) & (z + s + 1 < nz))
        def _():
            landed(z + s + 1)

        @pl.when(s == 0)
        def _():
            go_y(z).wait_recv()
            spread_edge(z)

        @pl.when((s > 0) & (z - s >= 0))
        def _():
            landed_edge(z - s)

        @pl.when((s > 0) & (z + s < nz))
        def _():
            landed_edge(z + s)

        @pl.when(s > 0)
        def _():
            rest_y(p).wait_recv()

        go_c(p, 1).start()

        @pl.when(s == 0)
        def _():
            for load in loads:
                load.wait()

            @pl.loop(1, n)
            def _(i):
                other = lax.rem(me + i, n)
                remote(ct.at[other], cs.at[other], cts.at[i], ctr.at[other], other).wait_recv()

        go_c(p, 0).wait_recv()
        go_c(p, 1).wait_recv()
        compute(p)

        @pl.loop(0, QUARTERS)
        def _(q):
            share(p, 1 - y, q).start()

        @pl.loop(0, QUARTERS)
        def _(q):
            share(p, y, q).start()

        @pl.when(s >= 1)
        def _():
            y_step(plane(s - 1))

        @pl.when(s >= 3)
        def _():
            z_step(s - 2)

    y_step(plane(nz - 1))
    for k in range(max(1, nz - 2), nz):
        z_step(k)

    lead = keep.at[z, 1 - y, pl.ds(0, piece)]

    @pl.when(z > 0)
    def _():
        share_edge(0, z).wait_recv()
        lead[...] += rze[0, z].astype(jnp.float32)

    @pl.when(z < nz - 1)
    def _():
        share_edge(1, z).wait_recv()
        lead[...] += rze[1, z].astype(jnp.float32)

    sy[z, 0:piece, :] = lead[...].astype(jnp.bfloat16)
    share_y(z, 0).start()

    @pl.loop(1, QUARTERS + 1)
    def _(turn):
        q = lax.rem(turn, QUARTERS)
        span = pl.ds(pl.multiple_of(q * piece, piece), piece)
        share_y(z, q).wait_recv()
        keep[z, y, span, :] += ry[z, span, :].astype(jnp.float32)

        @pl.when(z > 0)
        def _():
            share_z(0, z, q).wait_recv()
            keep[z, y, span, :] += rz[0, z, span, :].astype(jnp.float32)

        @pl.when(z < nz - 1)
        def _():
            share_z(1, z, q).wait_recv()
            keep[z, y, span, :] += rz[1, z, span, :].astype(jnp.float32)

        out[span, :] = keep[z, y, span, :].astype(jnp.bfloat16)

    @pl.loop(1, n)
    def _(i):
        ct_copy(i).wait_send()

    @pl.loop(0, nz)
    def _(p):
        @pl.when((p <= z) & (z + 1 < nz))
        def _():
            go_up(p).wait_send()

        @pl.when((p >= z) & (z > 0))
        def _():
            go_down(p).wait_send()

        @pl.when((p <= z) & (z + 1 < nz))
        def _():
            edge(p, eu_s, me + 4).wait_send()

        @pl.when((p >= z) & (z > 0))
        def _():
            edge(p, ed_s, me - 4).wait_send()

        @pl.when(p == z)
        def _():
            go_y(p).wait_send()

        @pl.when(p != z)
        def _():
            rest_y(p).wait_send()

        @pl.when(p > z)
        def _():
            share_edge(0, p).wait_send()

        @pl.when(p < z)
        def _():
            share_edge(1, p).wait_send()

        go_c(p, 0).wait_send()
        go_c(p, 1).wait_send()

        @pl.loop(0, QUARTERS)
        def _(q):
            share(p, 0, q).wait_send()
            share(p, 1, q).wait_send()

            @pl.when((q > 0) | (p == z))
            def _():
                share_y(p, q).wait_send()

            @pl.when(p > z)
            def _():
                share_z(0, p, q).wait_send()

            @pl.when(p < z)
            def _():
                share_z(1, p, q).wait_send()


def scratch(n, rows, model, units, pad, hot):
    nz = n // 4
    piece = rows // QUARTERS
    half, full = jnp.bfloat16, jnp.float32
    dma = pltpu.SemaphoreType.DMA
    return [
        pltpu.VMEM((nz, 4, rows, model), half),
        pltpu.VMEM((nz, 2, rows, model), full),
        pltpu.VMEM((nz, 2, rows, model), half),
        pltpu.VMEM((nz, 2, rows, model), half),
        pltpu.VMEM((nz, rows, model), half),
        pltpu.VMEM((nz, rows, model), half),
        pltpu.VMEM((2, nz, rows, model), half),
        pltpu.VMEM((2, nz, rows, model), half),
        pltpu.VMEM((model, units), half),
        pltpu.VMEM((model, units), half),
        pltpu.VMEM((units, model), half),
        pltpu.VMEM((3 * pad, model), half),
        pltpu.VMEM((4 * rows, units), half),
        pltpu.VMEM((4 * rows, pad), half),
        pltpu.VMEM((n, 8, rows), full),
        pltpu.VMEM((n, 8, rows), full),
        pltpu.VMEM((2, nz, piece, model), half),
        pltpu.VMEM((2, nz, piece, model), half),
        dma((3 + 3 * hot,)), dma, dma((n,)), dma((n,)),
        dma((nz,)), dma((nz,)), dma((nz,)), dma((nz,)), dma((nz,)), dma((nz, 2)), dma((nz, 2)),
        dma((nz, 2, QUARTERS)), dma((nz, 2, QUARTERS)),
        dma((nz, QUARTERS)), dma((nz, QUARTERS)),
        dma((2, nz, QUARTERS)), dma((2, nz, QUARTERS)),
        dma((nz,)), dma((nz,)), dma((nz,)), dma((2, nz)), dma((2, nz)),
    ]


def shards(tokens, w_gate, w_up, w_down, hot_gate, hot_up, hot_down, cold_routes, hot_pick, gates):
    n = lax.axis_size("expert")
    micro_count, local_tokens, model = tokens.shape
    rows = micro_count * local_tokens
    hot, units, part = hot_gate.shape[0], w_gate.shape[2], hot_gate.shape[2]
    pad = -(-hot * part // 128) * 128
    need = rows * model * n * 9 // 2 * 2 + 3 * model * (units + pad) * 2
    if n % 4 or part % 16 or rows % 64 or model % 256 or need > ROOM or hot > 7:
        return routed(
            tokens, w_gate, w_up, w_down, hot_gate, hot_up, hot_down, cold_routes, hot_pick, gates
        )
    anyplace = pl.BlockSpec(memory_space=pl.ANY)
    vmem = pl.BlockSpec(memory_space=pltpu.VMEM)
    mixed = pl.pallas_call(
        functools.partial(fused, n, hot, part),
        out_shape=jax.ShapeDtypeStruct((rows, model), jnp.bfloat16),
        in_specs=[anyplace, vmem, vmem, vmem] + [anyplace] * 6,
        out_specs=vmem,
        scratch_shapes=scratch(n, rows, model, units, pad, hot),
        compiler_params=pltpu.CompilerParams(
            collective_id=0, has_side_effects=True, vmem_limit_bytes=64 * 2**20 - 2**17
        ),
    )(
        tokens.reshape(rows, model), jnp.transpose(cold_routes, (2, 0, 1)), hot_pick,
        jnp.swapaxes(gates, 1, 2),
        w_gate[0], w_up[0], w_down[0],
        *(jnp.swapaxes(w, 1, 2) for w in (hot_gate, hot_up, hot_down)),
    )
    return mixed.reshape(tokens.shape)


def solution(mesh):
    in_specs = (
        P(None, ("groups", "expert"), None),
        P("expert", None, None),
        P("expert", None, None),
        P("expert", None, None),
        P(None, None, "expert"),
        P(None, None, "expert"),
        P(None, None, "expert"),
        P(None, ("groups", "expert"), None),
        P(None, ("groups", "expert")),
        P(None, ("groups", "expert"), None),
    )
    out_specs = P(None, ("groups", "expert"), None)
    return jax.shard_map(shards, mesh=mesh, in_specs=in_specs, out_specs=out_specs, check_vma=False)
```

```python
import functools

import jax
import jax.numpy as jnp
from jax import lax
from jax.experimental import pallas as pl
from jax.experimental.pallas import tpu as pltpu
from jax.sharding import PartitionSpec as P

TOP = 8
HOT = 2


def expert_rows(rows_in, weights):
    leading = rows_in.shape[:-1]
    flat_rows = rows_in.reshape(-1, rows_in.shape[-1])
    gate = jnp.dot(flat_rows, weights[0], preferred_element_type=jnp.float32)
    upward = jnp.dot(flat_rows, weights[1], preferred_element_type=jnp.float32)
    hidden = (jax.nn.silu(gate) * upward).astype(jnp.bfloat16)
    result = jnp.dot(hidden, weights[2], preferred_element_type=jnp.float32).astype(jnp.bfloat16)
    return result.reshape(leading + (result.shape[-1],))


def slot_table(routes_block, axis_width, capacity):
    expert = routes_block.reshape(-1)
    total_count = expert.shape[0]
    onehot = (expert[:, None] == jnp.arange(axis_width, dtype=jnp.int32)[None, :]).astype(jnp.int32)
    before = jnp.cumsum(onehot, axis=0) - onehot
    slot_rank = jnp.sum(before * onehot, axis=1)
    slot_place = expert * capacity + slot_rank
    target = jnp.arange(axis_width * capacity, dtype=jnp.int32)
    matched = slot_place[None, :] == target[:, None]
    filled = jnp.any(matched, axis=1)
    source = jnp.sum(
        jnp.where(matched, jnp.arange(total_count, dtype=jnp.int32)[None, :], 0), axis=1
    )
    return (slot_place, source, filled)


def routed(tokens, w_gate, w_up, w_down, hot_gate, hot_up, hot_down, cold_routes, hot_pick, gates):
    axis_width = lax.axis_size("expert")
    micro_count, local_tokens, model_width = tokens.shape
    picks = TOP - 1
    capacity = local_tokens * picks * 3 // (2 * axis_width) + 1
    own_weights = (w_gate[0], w_up[0], w_down[0])
    outbound = []
    tables = []
    for micro in range(micro_count):
        slot_place, source, filled = slot_table(cold_routes[micro], axis_width, capacity)
        rows_out = tokens[micro][source // picks]
        rows_out = jnp.where(filled[:, None], rows_out, jnp.zeros_like(rows_out))
        outbound.append(rows_out.reshape(axis_width, capacity, model_width))
        tables.append(slot_place)
    joined = jnp.concatenate(outbound, axis=1)
    back_all = lax.all_to_all(
        expert_rows(
            lax.all_to_all(joined, "expert", split_axis=0, concat_axis=0, tiled=True), own_weights
        ),
        "expert",
        split_axis=0,
        concat_axis=0,
        tiled=True,
    )
    returned = [
        back_all[:, micro * capacity : (micro + 1) * capacity] for micro in range(micro_count)
    ]
    cold_parts = []
    for micro in range(micro_count):
        picked = returned[micro].reshape(axis_width * capacity, model_width)[tables[micro]]
        picked = picked.reshape(local_tokens, picks, model_width).astype(jnp.float32)
        cold_parts.append(jnp.sum(picked * gates[micro, :, 1:, None], axis=1))
    cold_total = jnp.stack(cold_parts)
    all_rows = micro_count * local_tokens
    flat = tokens.reshape(all_rows, model_width)
    order = jnp.argsort(hot_pick.reshape(all_rows), stable=True)
    share = all_rows // HOT
    grouped = flat[order].reshape(HOT, share, model_width)
    gate = jnp.einsum(
        "hsd,hdf->hsf",
        grouped,
        lax.all_gather(hot_gate, "expert", axis=2, tiled=True),
        preferred_element_type=jnp.float32,
    )
    upward = jnp.einsum(
        "hsd,hdf->hsf",
        grouped,
        lax.all_gather(hot_up, "expert", axis=2, tiled=True),
        preferred_element_type=jnp.float32,
    )
    hidden = (jax.nn.silu(gate) * upward).astype(jnp.bfloat16)
    hot_sum = jnp.einsum(
        "hsf,hdf->hsd",
        hidden,
        lax.all_gather(hot_down, "expert", axis=2, tiled=True),
        preferred_element_type=jnp.float32,
    )
    sorted_out = hot_sum.astype(jnp.bfloat16).reshape(all_rows, model_width)
    inverse = jnp.argsort(order)
    hot_out = sorted_out[inverse].astype(jnp.float32) * gates[:, :, 0].reshape(all_rows)[:, None]
    total = hot_out.reshape(micro_count, local_tokens, model_width) + cold_total
    return total.astype(jnp.bfloat16)


QUARTERS = 4
ROOM = 56 * 2**20


def column(row):
    rows = row.shape[1]
    down = lax.broadcasted_iota(jnp.int32, (rows, rows), 0)
    across = lax.broadcasted_iota(jnp.int32, (rows, rows), 1)
    return jnp.sum(jnp.where(down == across, row, 0.0), axis=1, keepdims=True)


def fused(
    n, hot, part, tok, routes, pick, gts, wg_in, wu_in, wd_in, hg_in, hu_in, hd_in, out,
    xs, keep, sc, rc, sy, ry, sz, rz, wg, wu, wd, wh, hid, hhid, cs, ct,
    wsem, tsem, cts, ctr, up_s, down_s, z_r, y_s, y_r, c_s, c_r,
    rc_s, rc_r, ry_s, ry_r, rz_s, rz_r,
):
    nz = n // 4
    rows, model = tok.shape
    units = wg.shape[1]
    pad = hhid.shape[1]
    piece = rows // QUARTERS
    me = lax.axis_index("expert")
    c = lax.rem(me, 2)
    y = lax.rem(lax.div(me, 2), 2)
    z = lax.div(me, 4)
    own = y * 2 + c
    side = (1 - y) * 2 + c
    peer_y = z * 4 + side
    peer_c = z * 4 + y * 2 + (1 - c)

    def remote(src, dst, send, recv, device):
        return pltpu.make_async_remote_copy(
            src_ref=src, dst_ref=dst, send_sem=send, recv_sem=recv,
            device_id={"expert": device}, device_id_type=pl.DeviceIdType.MESH,
        )

    loads = [
        pltpu.make_async_copy(src, dst, wsem.at[i])
        for i, (src, dst) in enumerate((
            *(
                (src.at[h], wh.at[pl.ds(t * pad + h * part, part)])
                for t, src in enumerate((hg_in, hu_in, hd_in)) for h in range(hot)
            ),
            (wg_in, wg), (wu_in, wu), (wd_in, wd),
        ))
    ]
    first = pltpu.make_async_copy(tok, xs.at[z, own], tsem)
    first.start()
    for load in loads:
        load.start()

    barrier = pltpu.get_barrier_semaphore()

    @pl.loop(1, n)
    def _(i):
        pl.semaphore_signal(
            barrier, inc=1, device_id={"expert": lax.rem(me + i, n)},
            device_id_type=pl.DeviceIdType.MESH,
        )

    pl.semaphore_wait(barrier, n - 1)

    def ct_copy(i):
        peer = lax.rem(me + i, n)
        return remote(ct.at[peer], cs.at[me], cts.at[i], ctr.at[me], peer)

    def go_up(p):
        return remote(xs.at[p, own], xs.at[p, own], up_s.at[p], z_r.at[p], me + 4)

    def go_down(p):
        return remote(xs.at[p, own], xs.at[p, own], down_s.at[p], z_r.at[p], me - 4)

    def go_y(p):
        return remote(xs.at[p, own], xs.at[p, own], y_s.at[p], y_r.at[p], peer_y)

    def go_c(p, which):
        slot = own if which == 0 else side
        return remote(
            xs.at[p, slot], xs.at[p, slot], c_s.at[p, which], c_r.at[p, which], peer_c
        )

    def spread(p):
        @pl.when((p <= z) & (z + 1 < nz))
        def _():
            go_up(p).start()

        @pl.when((p >= z) & (z > 0))
        def _():
            go_down(p).start()

    def landed(p):
        remote(xs.at[p, own], xs.at[p, own], up_s.at[p], z_r.at[p], me).wait_recv()
        spread(p)
        go_y(p).start()
        go_c(p, 0).start()

    def plane(s):
        near = jnp.minimum(z, nz - 1 - z)
        step = lax.div(s + 1, 2)
        both = jnp.where(lax.rem(s, 2) == 1, z - step, z + step)
        far = jnp.where(z * 2 < nz, s, nz - 1 - s)
        return jnp.where(s <= 2 * near, both, far)

    def share(p, j, q):
        span = pl.ds(pl.multiple_of(q * piece, piece), piece)
        return remote(
            sc.at[p, j, span], rc.at[p, j, span], rc_s.at[p, j, q], rc_r.at[p, j, q], peer_c
        )

    def share_y(p, q):
        span = pl.ds(pl.multiple_of(q * piece, piece), piece)
        return remote(sy.at[p, span], ry.at[p, span], ry_s.at[p, q], ry_r.at[p, q], peer_y)

    def share_z(way, p, q):
        span = pl.ds(pl.multiple_of(q * piece, piece), piece)
        return remote(
            sz.at[way, p, span], rz.at[way, p, span], rz_s.at[way, p, q], rz_r.at[way, p, q],
            jnp.where(way == 0, me + 4, me - 4),
        )

    def compute(p):
        wide = 256 if units % 256 == 0 else units
        x = xs.at[p]
        cold_c = jnp.concatenate([column(cs[p * 4 + j, 0:1, :]) for j in range(4)], axis=0)

        @pl.loop(0, units // wide)
        def _(k):
            cols = pl.ds(pl.multiple_of(k * wide, wide), wide)
            v = x[...].reshape(4 * rows, model)
            g = jnp.dot(v, wg[:, cols], preferred_element_type=jnp.float32)
            u = jnp.dot(v, wu[:, cols], preferred_element_type=jnp.float32)
            hid[:, cols] = (g / (1.0 + jnp.exp(-g)) * u).astype(jnp.bfloat16)

        v = x[...].reshape(4 * rows, model)
        gu = lax.dot_general(
            v, wh[: 2 * pad, :], (((1,), (1,)), ((), ())), preferred_element_type=jnp.float32
        )
        g, u = gu[:, :pad], gu[:, pad:]
        lane = lax.broadcasted_iota(jnp.int32, (rows, pad), 1)
        warm = []
        for j in range(4):
            scale = jnp.zeros((rows, pad), jnp.float32)
            for h in range(hot):
                weight = column(cs[p * 4 + j, 1 + h : 2 + h, :])
                scale = jnp.where((lane >= h * part) & (lane < (h + 1) * part), weight, scale)
            warm.append(scale)
        warm = jnp.concatenate(warm, axis=0)
        hhid[...] = (g / (1.0 + jnp.exp(-g)) * u * warm).astype(jnp.bfloat16)

        tile = 512 if model % 512 == 0 else model

        @pl.loop(0, model // tile)
        def _(k):
            cols = pl.ds(pl.multiple_of(k * tile, tile), tile)
            r = jnp.dot(hid[...], wd[:, cols], preferred_element_type=jnp.float32)
            r = r.astype(jnp.bfloat16).astype(jnp.float32) * cold_c
            r = r + jnp.dot(hhid[...], wh[2 * pad :, cols], preferred_element_type=jnp.float32)
            for j in range(2):
                low = r[2 * j * rows : (2 * j + 1) * rows]
                high = r[(2 * j + 1) * rows : (2 * j + 2) * rows]
                keep[p, j, :, cols] = jnp.where(c == 0, low, high)
                sc[p, j, :, cols] = jnp.where(c == 0, high, low).astype(jnp.bfloat16)

    def y_step(p):
        @pl.loop(0, QUARTERS)
        def _(q):
            span = pl.ds(pl.multiple_of(q * piece, piece), piece)
            share(p, 1 - y, q).wait_recv()
            total = keep[p, 1 - y, span, :] + rc[p, 1 - y, span, :].astype(jnp.float32)
            sy[p, span, :] = total.astype(jnp.bfloat16)
            share_y(p, q).start()

        @pl.loop(0, QUARTERS)
        def _(q):
            span = pl.ds(pl.multiple_of(q * piece, piece), piece)
            share(p, y, q).wait_recv()
            keep[p, y, span, :] += rc[p, y, span, :].astype(jnp.float32)

    def z_step(k):
        @pl.loop(0, 2)
        def _(turn):
            way = jnp.where(z * 2 < nz, turn, 1 - turn)
            p = jnp.where(way == 0, k, nz - 1 - k)
            active = jnp.where(way == 0, z < k, z > nz - 1 - k)
            fed = jnp.where(way == 0, z > 0, z < nz - 1)

            @pl.when(active)
            def _():
                @pl.loop(0, QUARTERS)
                def _(q):
                    span = pl.ds(pl.multiple_of(q * piece, piece), piece)
                    share_y(p, q).wait_recv()
                    keep[p, y, span, :] += ry[p, span, :].astype(jnp.float32)

                    @pl.when(fed)
                    def _():
                        share_z(way, p, q).wait_recv()
                        keep[p, y, span, :] += rz[way, p, span, :].astype(jnp.float32)

                    sz[way, p, span, :] = keep[p, y, span, :].astype(jnp.bfloat16)
                    share_z(way, p, q).start()

    first.wait()
    spread(z)
    go_y(z).start()
    go_c(z, 0).start()

    if pad > hot * part:
        for t in range(3):
            blank = wh.at[pl.ds(t * pad + hot * part, pad - hot * part)]
            blank[...] = jnp.zeros_like(blank)

    ct[...] = jnp.zeros_like(ct)
    micros = gts.shape[0]

    def joined(parts):
        return jnp.concatenate(parts, axis=1)

    warm_row = joined([gts[m, 0:1, :] for m in range(micros)])
    chosen = joined([pick[m : m + 1, :] for m in range(micros)])
    named = [
        (
            joined([routes[k, m : m + 1, :] for m in range(micros)]),
            joined([gts[m, k + 1 : k + 2, :] for m in range(micros)]),
        )
        for k in range(routes.shape[0])
    ]

    def row(e):
        return sum(jnp.where(route == e, weight, 0.0) for route, weight in named)

    for e in range(n):
        ct[e, 0:1, :] = row(e)
        for h in range(hot):
            ct[e, 1 + h : 2 + h, :] = jnp.where(chosen == h, warm_row, 0.0)

    @pl.loop(1, n)
    def _(i):
        ct_copy(i).start()

    cs[me] = ct[me]

    @pl.loop(0, nz)
    def _(s):
        p = plane(s)

        @pl.when((s + 1 < nz) & (z - s - 1 >= 0))
        def _():
            landed(z - s - 1)

        @pl.when((s + 1 < nz) & (z + s + 1 < nz))
        def _():
            landed(z + s + 1)

        go_y(p).wait_recv()
        go_c(p, 1).start()

        @pl.when(s == 0)
        def _():
            for load in loads:
                load.wait()

            @pl.loop(1, n)
            def _(i):
                other = lax.rem(me + i, n)
                remote(ct.at[other], cs.at[other], cts.at[i], ctr.at[other], other).wait_recv()

        go_c(p, 0).wait_recv()
        go_c(p, 1).wait_recv()
        compute(p)

        @pl.loop(0, QUARTERS)
        def _(q):
            share(p, 1 - y, q).start()

        @pl.loop(0, QUARTERS)
        def _(q):
            share(p, y, q).start()

        @pl.when(s >= 1)
        def _():
            y_step(plane(s - 1))

        @pl.when(s >= 3)
        def _():
            z_step(s - 2)

    y_step(plane(nz - 1))
    for k in range(max(1, nz - 2), nz):
        z_step(k)

    @pl.loop(0, QUARTERS)
    def _(q):
        span = pl.ds(pl.multiple_of(q * piece, piece), piece)
        share_y(z, q).wait_recv()
        keep[z, y, span, :] += ry[z, span, :].astype(jnp.float32)

        @pl.when(z > 0)
        def _():
            share_z(0, z, q).wait_recv()
            keep[z, y, span, :] += rz[0, z, span, :].astype(jnp.float32)

        @pl.when(z < nz - 1)
        def _():
            share_z(1, z, q).wait_recv()
            keep[z, y, span, :] += rz[1, z, span, :].astype(jnp.float32)

        out[span, :] = keep[z, y, span, :].astype(jnp.bfloat16)

    @pl.loop(1, n)
    def _(i):
        ct_copy(i).wait_send()

    @pl.loop(0, nz)
    def _(p):
        @pl.when((p <= z) & (z + 1 < nz))
        def _():
            go_up(p).wait_send()

        @pl.when((p >= z) & (z > 0))
        def _():
            go_down(p).wait_send()

        go_y(p).wait_send()
        go_c(p, 0).wait_send()
        go_c(p, 1).wait_send()

        @pl.loop(0, QUARTERS)
        def _(q):
            share(p, 0, q).wait_send()
            share(p, 1, q).wait_send()
            share_y(p, q).wait_send()

            @pl.when(p > z)
            def _():
                share_z(0, p, q).wait_send()

            @pl.when(p < z)
            def _():
                share_z(1, p, q).wait_send()


def scratch(n, rows, model, units, pad, hot):
    nz = n // 4
    half, full = jnp.bfloat16, jnp.float32
    dma = pltpu.SemaphoreType.DMA
    return [
        pltpu.VMEM((nz, 4, rows, model), half),
        pltpu.VMEM((nz, 2, rows, model), full),
        pltpu.VMEM((nz, 2, rows, model), half),
        pltpu.VMEM((nz, 2, rows, model), half),
        pltpu.VMEM((nz, rows, model), half),
        pltpu.VMEM((nz, rows, model), half),
        pltpu.VMEM((2, nz, rows, model), half),
        pltpu.VMEM((2, nz, rows, model), half),
        pltpu.VMEM((model, units), half),
        pltpu.VMEM((model, units), half),
        pltpu.VMEM((units, model), half),
        pltpu.VMEM((3 * pad, model), half),
        pltpu.VMEM((4 * rows, units), half),
        pltpu.VMEM((4 * rows, pad), half),
        pltpu.VMEM((n, 8, rows), full),
        pltpu.VMEM((n, 8, rows), full),
        dma((3 + 3 * hot,)), dma, dma((n,)), dma((n,)),
        dma((nz,)), dma((nz,)), dma((nz,)), dma((nz,)), dma((nz,)), dma((nz, 2)), dma((nz, 2)),
        dma((nz, 2, QUARTERS)), dma((nz, 2, QUARTERS)),
        dma((nz, QUARTERS)), dma((nz, QUARTERS)),
        dma((2, nz, QUARTERS)), dma((2, nz, QUARTERS)),
    ]


def shards(tokens, w_gate, w_up, w_down, hot_gate, hot_up, hot_down, cold_routes, hot_pick, gates):
    n = lax.axis_size("expert")
    micro_count, local_tokens, model = tokens.shape
    rows = micro_count * local_tokens
    hot, units, part = hot_gate.shape[0], w_gate.shape[2], hot_gate.shape[2]
    pad = -(-hot * part // 128) * 128
    need = rows * model * n * 9 // 2 * 2 + 3 * model * (units + pad) * 2
    if n % 4 or part % 16 or rows % 64 or model % 256 or need > ROOM or hot > 7:
        return routed(
            tokens, w_gate, w_up, w_down, hot_gate, hot_up, hot_down, cold_routes, hot_pick, gates
        )
    anyplace = pl.BlockSpec(memory_space=pl.ANY)
    vmem = pl.BlockSpec(memory_space=pltpu.VMEM)
    mixed = pl.pallas_call(
        functools.partial(fused, n, hot, part),
        out_shape=jax.ShapeDtypeStruct((rows, model), jnp.bfloat16),
        in_specs=[anyplace, vmem, vmem, vmem] + [anyplace] * 6,
        out_specs=vmem,
        scratch_shapes=scratch(n, rows, model, units, pad, hot),
        compiler_params=pltpu.CompilerParams(
            collective_id=0, has_side_effects=True, vmem_limit_bytes=64 * 2**20 - 2**17
        ),
    )(
        tokens.reshape(rows, model), jnp.transpose(cold_routes, (2, 0, 1)), hot_pick,
        jnp.swapaxes(gates, 1, 2),
        w_gate[0], w_up[0], w_down[0],
        *(jnp.swapaxes(w, 1, 2) for w in (hot_gate, hot_up, hot_down)),
    )
    return mixed.reshape(tokens.shape)


def solution(mesh):
    in_specs = (
        P(None, ("groups", "expert"), None),
        P("expert", None, None),
        P("expert", None, None),
        P("expert", None, None),
        P(None, None, "expert"),
        P(None, None, "expert"),
        P(None, None, "expert"),
        P(None, ("groups", "expert"), None),
        P(None, ("groups", "expert")),
        P(None, ("groups", "expert"), None),
    )
    out_specs = P(None, ("groups", "expert"), None)
    return jax.shard_map(shards, mesh=mesh, in_specs=in_specs, out_specs=out_specs, check_vma=False)
```
